32 devices in a mesh: pipe: 4 (over x, core), expert: 4 (over z), tensor: 2 (over y).
Axes of the slice: x: 2, y: 2, z: 4, core: 2. Of those that a mesh axis runs over, the one named last changes fastest.
Arguments:
- stream: bfloat16 [2, 4, 64, 7168], P(None, 'pipe', 'expert', 'tensor'), may hold values from -6 to 6
- expert_ids: int32 [2, 4, 64, 2], P(None, 'pipe', 'expert'), may hold values from 0 to 3, all different within a row; in each aligned block of 16 rows (0 to 15, 16 to 31, ..., all dimensions but the last counted through in order) at most 12 rows name the same one
- norm_gain: float32 [4, 7168], P('pipe', 'tensor'), may hold values from 0.1 to 1.9
- router: float32 [4, 7168, 4], P('pipe', 'tensor'), may hold values from -0.0625 to 0.0625
- w_up: bfloat16 [4, 7168, 1024], P('expert', 'tensor'), may hold values from -0.0625 to 0.0625
- w_down: bfloat16 [4, 1024, 7168], P('expert', None, 'tensor'), may hold values from -0.1875 to 0.1875
Outputs:
- result: bfloat16 [2, 4, 64, 7168], P(None, 'pipe', 'expert', 'tensor')
The draws below stay inside these ranges and needn't reach their ends.
Inputs may be any that keep to these rules, and one draw needn't show every extreme that they name: `expert_ids`: each token names 2 different experts. Among the 16 tokens of one direction held by one index of the expert axis at one section, at most 12 name any one expert, and in every draw some expert is named by exactly 12 of them.
All inputs are finite; a program needn't handle non-finite values.
Results may differ from the reference program's by a relative error of at most 0.0065.
Values may be sent and summed in bfloat16 or wider, within the bound.
A program may use at most 64 MiB of HBM per device.

```python
import math
import jax
import jax.numpy as jnp
import numpy as np
from jax import lax

D = 7168
FF = 1024
TOK_DEV = 16
PIPE = 4
EXPERTS = 4
TOP = 2
TOKENS = 64
CAP = 12
N_EXPERT = 4


def shard_levels(stream_key, extent, split, smallest, top_value):
    factor_of, own = 1.0, jax.random.fold_in(stream_key, 6)
    for position, blocks in split:
        draws = jnp.exp(jax.random.uniform(jax.random.fold_in(own, position), (blocks,), jnp.float32, smallest / len(split), top_value / len(split)))
        factor_of = factor_of * jnp.repeat(draws, extent[position] // blocks).reshape([-1 if axis == position else 1 for axis in range(len(extent))])
    return factor_of


def shared_out(own_key, own, number, rows, count, top, bound, skew):
    order = jax.random.permutation(own_key, count)
    heavy_load, usual = shares(count, rows * top, bound, skew, True), shares(count, rows * top, bound, skew, False)
    places = jnp.arange(count)

    def named(lengths, rotation):
        used = int((lengths > 0).sum())
        fixed = max(1, used // 4)
        moved = fixed + (places - fixed + rotation * (used - fixed)) % max(1, count - fixed)
        return jnp.zeros((count,), jnp.int32).at[order[jnp.where(places < fixed, places, moved)]].set(jnp.asarray(lengths, jnp.int32))

    lengths = jnp.where(number % 4 == 0, named(heavy_load, number // 4), named(usual, number - number // 4 - 1))
    mixed = jax.random.permutation(jax.random.fold_in(own, 3), count)
    source_of, sink = mixed[0:count // 2 * 2:2], mixed[1:count // 2 * 2:2]
    slack = jnp.minimum(lengths[source_of] - 1, bound - lengths[sink]) // 2
    slack = jnp.where((source_of == order[0]) | (sink == order[0]) | (lengths[sink] == 0), 0, jnp.maximum(slack, 0))
    moved = jax.random.randint(jax.random.fold_in(own, 4), (count // 2,), 0, 1 << 20) % (slack + 1)
    lengths = lengths.at[source_of].add(-moved).at[sink].add(moved)
    items = jnp.searchsorted(jnp.cumsum(lengths), jnp.arange(rows * top), side="right").astype(jnp.int32)
    listing = items.reshape(top, rows).T
    listing = listing[jax.random.permutation(jax.random.fold_in(own, 1), rows)]
    rotation = jax.random.randint(jax.random.fold_in(own, 2), (rows, 1), 0, top)
    return jnp.take_along_axis(listing, (jnp.arange(top)[None, :] + rotation) % top, axis=1)


def shares(count, total, limit, lean, full):
    portions = [(1 << 20) // math.isqrt(grade ** lean) + 1 for grade in range(1, count + 1)]
    largest = limit if full else min(limit, max(-(-total // count), total * portions[0] // sum(portions)))
    least = 1 if total - largest >= count - 1 else 0
    counts, rest = [largest] + [least] * (count - 1), total - largest - least * (count - 1)
    while rest > 0:
        free = [i for i in range(1, count) if counts[i] < largest] or [i for i in range(1, count) if counts[i] < limit]
        mass, budget = sum([portions[i] for i in free]), rest
        for i in free:
            addition = min(limit - counts[i], max(1, budget * portions[i] // mass), rest)
            counts[i] = counts[i] + addition
            rest = rest - addition
    return np.array(counts)


def scatter_about(own_key, extent, scale, most, split=(), held_as=jnp.bfloat16):
    loudness = shard_levels(own_key, extent, split, -0.22, 0.18) if split else 1.0
    values = jax.random.normal(own_key, extent, jnp.float32) * scale * loudness
    return jnp.minimum(jnp.maximum(values, -most), most).astype(held_as)


def setup_inputs(seed: int = 0) -> dict:
    splits = jax.random.split(jax.random.key(seed), 7)
    stream = scatter_about(splits[0], (2, PIPE, TOKENS, D), 1.0, 6.0, ((1, 4), (2, 4), (3, 2)))
    expert_ids_keys = jax.random.split(jax.random.fold_in(splits[1], 1), 2 * PIPE * TOKENS // TOK_DEV)
    expert_ids_turns = jax.random.permutation(jax.random.fold_in(splits[1], 3), 2 * PIPE * TOKENS // TOK_DEV)
    expert_ids = jax.vmap(lambda own, number: shared_out(jax.random.fold_in(splits[1], 2), own, number, TOK_DEV, EXPERTS, TOP, CAP, 2))(expert_ids_keys, expert_ids_turns).reshape((2, PIPE, TOKENS, TOP))
    norm_gain = jnp.clip(1.0 + 0.18 * jax.random.normal(splits[2], (PIPE, D), jnp.float32), 0.1, 1.9)
    router = scatter_about(splits[3], (PIPE, D, EXPERTS), D ** -0.5, 0.0625, ((0, 4), (1, 2)), jnp.float32)
    w_up = scatter_about(splits[4], (EXPERTS, D, FF), D ** -0.5, 0.0625, ((0, 4), (1, 2)))
    w_down = scatter_about(splits[5], (EXPERTS, FF, D), FF ** -0.5, 0.1875, ((0, 4), (2, 2)))
    return dict(stream=stream, expert_ids=expert_ids, norm_gain=norm_gain, router=router, w_up=w_up, w_down=w_down)


norm_eps = 1e-06
route_scale = 2.5

def reference(stream, expert_ids, norm_gain, router, w_up, w_down):
    ahead = jnp.roll(stream[0], 1, axis=0)
    behind = jnp.roll(stream[1], -1, axis=0)
    arrived = jnp.stack([ahead, behind]).astype(jnp.float32)
    inverse = lax.rsqrt(lax.optimization_barrier(jnp.mean(arrived * arrived, axis=-1)) + norm_eps)
    normed = arrived * norm_gain[None, :, None, :] * inverse[..., None]
    logits = jnp.einsum('dptc,pce->dpte', normed, router, precision=lax.Precision.HIGHEST)
    picked = jnp.take_along_axis(logits, expert_ids, axis=-1)
    scores = jax.nn.sigmoid(picked)
    gates = route_scale * scores / lax.optimization_barrier(jnp.sum(scores, axis=-1, keepdims=True))
    hidden = normed.astype(jnp.bfloat16)
    groups = expert_ids.reshape(2, PIPE, N_EXPERT, TOK_DEV * TOP)
    onehot = (groups[..., None] == jnp.arange(EXPERTS, dtype=jnp.int32)).astype(jnp.int32)
    earlier = jnp.cumsum(onehot, axis=3) - onehot
    within = lax.optimization_barrier(jnp.sum(earlier * onehot, axis=-1))
    heading = lax.broadcasted_iota(jnp.int32, groups.shape, 0)
    section = lax.broadcasted_iota(jnp.int32, groups.shape, 1)
    member = lax.broadcasted_iota(jnp.int32, groups.shape, 2)
    entry = lax.broadcasted_iota(jnp.int32, groups.shape, 3)
    place = ((section * N_EXPERT + member) * 2 + heading) * CAP + within
    anchor = ((heading * PIPE + section) * N_EXPERT + member) * TOK_DEV + entry // TOP
    length = PIPE * N_EXPERT * 2 * CAP
    owner = jnp.full((EXPERTS, length), 2 * PIPE * TOKENS, jnp.int32).at[groups, place].set(anchor)
    width = hidden.shape[-1]
    table = jnp.concatenate([hidden.reshape(-1, width), jnp.zeros((1, width), jnp.bfloat16)], axis=0)

    def expert_rows(pieces):
        owned, upper, lower = pieces
        inner = jnp.dot(table[owned], upper, preferred_element_type=jnp.float32)
        active = jax.nn.silu(inner).astype(jnp.bfloat16)
        return jnp.dot(active, lower, preferred_element_type=jnp.float32).astype(jnp.bfloat16)
    produced = lax.map(expert_rows, (owner, w_up, w_down))

    def combine(pieces):
        chosen, spots, weights = pieces
        rows = produced[chosen, spots].astype(jnp.float32)
        rows = rows.reshape(N_EXPERT * TOK_DEV, TOP, width)
        return jnp.einsum('tk,tkc->tc', weights, rows)
    mixed = lax.map(combine, (groups.reshape(2 * PIPE, N_EXPERT, TOK_DEV * TOP), place.reshape(2 * PIPE, N_EXPERT, TOK_DEV * TOP), gates.reshape(2 * PIPE, TOKENS, TOP)))
    result = arrived + mixed.reshape(arrived.shape)
    return result.astype(jnp.bfloat16)
```

```python
import functools

import jax
import jax.numpy as jnp
from jax import lax
from jax.experimental import pallas as pl
from jax.experimental.pallas import tpu as pltpu
from jax.sharding import PartitionSpec as P

norm_eps = 1e-06
route_scale = 2.5
MESH = pl.DeviceIdType.MESH


def pieces_of(width, most):
    for count in range(most, 0, -1):
        if width % (count * 128) == 0:
            return count
    return 1


def layer(
    sizes, slots, feat, cols,
    stream, ids_ref, gain_hbm, router_ref, up_hbm, down_hbm, out_ref,
    up, down, arrived, send, recv, rows32, inner, part, parts_in, active, squares, squares_in,
    small, small_in, ret, back, weights, gain_ref,
    load_sem, shift_send, shift_recv, disp_send, disp_recv, ten_send, ten_recv, ret_send, ret_recv,
):
    n_pipe, n_exp, n_ten = sizes
    pipe, expert, tensor = lax.axis_index("pipe"), lax.axis_index("expert"), lax.axis_index("tensor")
    tokens, width = arrived.shape
    half = tokens // 2
    hidden_units = up.shape[1]
    experts = router_ref.shape[0]
    step_f, step_c = width // feat, hidden_units // cols

    def section(by):
        return (lax.rem(pipe + by + n_pipe, n_pipe), expert, tensor)

    def member(by):
        return (pipe, lax.rem(expert + by + n_exp, n_exp), tensor)

    def holder(by):
        return (pipe, expert, lax.rem(tensor + by + n_ten, n_ten))

    barrier = pltpu.get_barrier_semaphore()
    greeted = [section(1), section(-1)]
    greeted += [member(o) for o in range(1, n_exp)] + [holder(o) for o in range(1, n_ten)]
    for who in greeted:
        pl.semaphore_signal(barrier, inc=1, device_id=who, device_id_type=MESH)

    loads = []
    for f in range(feat):
        at = pl.ds(f * step_f, step_f)
        loads.append(pltpu.make_async_copy(up_hbm.at[0, at], up.at[at], load_sem.at[f]))
    loads.append(pltpu.make_async_copy(down_hbm.at[0], down, load_sem.at[feat]))
    gain_load = pltpu.make_async_copy(
        gain_hbm, gain_ref.at[:, pl.ds(0, width)], load_sem.at[feat + 1]
    )
    gain_load.start()
    for load in loads:
        load.start()
    pl.semaphore_wait(barrier, len(greeted))

    shifts = [
        pltpu.make_async_remote_copy(
            src_ref=stream.at[d, 0], dst_ref=arrived.at[pl.ds(d * half, half)],
            send_sem=shift_send.at[d], recv_sem=shift_recv.at[d],
            device_id=section(1 - 2 * d), device_id_type=MESH,
        )
        for d in range(2)
    ]
    for copy in shifts:
        copy.start()

    ids = ids_ref[...]
    total = n_exp * slots
    lane = lax.broadcasted_iota(jnp.int32, (tokens, total), 1)
    block = lane // slots
    lane_expert = lax.rem(block + expert, n_exp)
    takes = jnp.zeros((tokens, total), jnp.float32)
    for k in range(ids.shape[1]):
        takes += jnp.where(ids[:, k : k + 1] == lane_expert, 1.0, 0.0)
    below = lax.broadcasted_iota(jnp.int32, (tokens, tokens), 0) > lax.broadcasted_iota(
        jnp.int32, (tokens, tokens), 1
    )
    rank = jnp.dot(
        jnp.where(below, 1.0, 0.0).astype(jnp.bfloat16),
        takes.astype(jnp.bfloat16),
        preferred_element_type=jnp.float32,
    )
    spot = (lane - block * slots).astype(jnp.float32)
    place = jnp.where((rank == spot) & (takes > 0.0), 1.0, 0.0)
    pick = place.astype(jnp.bfloat16)

    for copy in shifts:
        copy.wait_recv()

    dispatch = {}
    for f in range(feat):
        at = pl.ds(f * step_f, step_f)
        taken = lax.dot_general(
            pick, arrived[:, at], (((0,), (0,)), ((), ())), preferred_element_type=jnp.float32
        ).astype(jnp.float32)
        for o in list(range(1, n_exp)) + [0]:
            rows = taken[o * slots : (o + 1) * slots].astype(jnp.bfloat16)
            if o == 0:
                recv[0, 0:slots, at] = rows
                continue
            send[o, 0:slots, at] = rows
            dispatch[o, f] = pltpu.make_async_remote_copy(
                src_ref=send.at[o, pl.ds(0, slots), at], dst_ref=recv.at[o, pl.ds(0, slots), at],
                send_sem=disp_send.at[o, f], recv_sem=disp_recv.at[o, f],
                device_id=member(o), device_id_type=MESH,
            )
            dispatch[o, f].start()

    gain_load.wait()
    held = arrived[...].astype(jnp.float32)
    small[0] = jnp.broadcast_to(jnp.sum(held * held, axis=1, keepdims=True), (tokens, 128))
    small[1] = jnp.zeros((tokens, 128), jnp.float32)
    small[1, :, 0:experts] = lax.dot_general(
        held * gain_ref[:, 0:width], router_ref[...], (((1,), (1,)), ((), ())),
        preferred_element_type=jnp.float32, precision=lax.Precision.HIGHEST,
    )

    def to_holders(src, dst, sem):
        copies = [
            pltpu.make_async_remote_copy(
                src_ref=src, dst_ref=dst(o), send_sem=ten_send.at[o, sem], recv_sem=ten_recv.at[o, sem],
                device_id=holder(o), device_id_type=MESH,
            )
            for o in range(1, n_ten)
        ]
        for copy in copies:
            copy.start()
        return copies

    small_copies = to_holders(small, lambda o: small_in.at[o], cols)

    square = jnp.zeros((total, 1), jnp.float32)
    for f in range(feat):
        at = pl.ds(f * step_f, step_f)
        gain = gain_ref[:, at]
        for o in range(n_exp):
            if o > 0:
                dispatch[o, f].wait_recv()
            rows32[pl.ds(o * slots, slots), :] = recv[o, 0:slots, at].astype(jnp.float32)
        rows = rows32[...]
        square += jnp.sum(rows * rows, axis=1, keepdims=True)
        if f == feat - 1:
            squares[...] = jnp.broadcast_to(square, (total, 128))
            square_copies = to_holders(squares, lambda o: squares_in.at[o], cols + 1)
        lifted = (rows * gain).astype(jnp.bfloat16)
        loads[f].wait()
        if f < feat - 1:
            found = jnp.dot(lifted, up[at, :], preferred_element_type=jnp.float32)
            if f == 0:
                inner[...] = found
            else:
                inner[...] += found
    exchange = []
    for c in range(cols):
        units = pl.ds(c * step_c, step_c)
        found = jnp.dot(lifted, up[at, units], preferred_element_type=jnp.float32)
        if feat > 1:
            found += inner[:, units]
        inner[:, units] = found
        part[c] = found.astype(jnp.bfloat16)
        exchange.append(to_holders(part.at[c], lambda o, c=c: parts_in.at[o, c], c))

    for copy in small_copies:
        copy.wait_recv()
    sums, logits = small[0], small[1, :, 0:experts]
    for o in range(1, n_ten):
        sums = sums + small_in[o, 0]
        logits = logits + small_in[o, 1, :, 0:experts]
    full = float(width * n_ten)
    logits = logits * lax.rsqrt(sums[:, 0:1] / full + norm_eps)
    which = lax.broadcasted_iota(jnp.int32, logits.shape, 1)
    scores = []
    for k in range(ids.shape[1]):
        picked = jnp.sum(jnp.where(ids[:, k : k + 1] == which, logits, 0.0), axis=1, keepdims=True)
        scores.append(1.0 / (1.0 + jnp.exp(-picked)))
    norm = scores[0]
    for score in scores[1:]:
        norm = norm + score
    gate = jnp.zeros((tokens, total), jnp.float32)
    for k, score in enumerate(scores):
        gate += jnp.where(ids[:, k : k + 1] == lane_expert, route_scale * score / norm, 0.0)
    gate = gate * place
    coarse = gate.astype(jnp.bfloat16)
    weights[0, :, 0:total] = coarse
    weights[1, :, 0:total] = (gate - coarse.astype(jnp.float32)).astype(jnp.bfloat16)

    for copy in square_copies:
        copy.wait_recv()
    total_sq = squares[...]
    for o in range(1, n_ten):
        total_sq = total_sq + squares_in[o]
    inverse = lax.rsqrt(total_sq[:, 0:1] / full + norm_eps)
    for c in range(cols):
        units = pl.ds(c * step_c, step_c)
        for copy in exchange[c]:
            copy.wait_recv()
        value = inner[:, units]
        for o in range(1, n_ten):
            value = value + parts_in[o, c].astype(jnp.float32)
        value = value * inverse
        active[:, units] = (value / (1.0 + jnp.exp(-value))).astype(jnp.bfloat16)

    loads[feat].wait()
    returns = {}
    for f in range(feat):
        at = pl.ds(f * step_f, step_f)
        made = jnp.dot(active[...], down[:, at], preferred_element_type=jnp.float32)
        for o in list(range(1, n_exp)) + [0]:
            rows = made[o * slots : (o + 1) * slots].astype(jnp.bfloat16)
            if o == 0:
                back[0, 0:slots, at] = rows
                continue
            ret[o, 0:slots, at] = rows
            returns[o, f] = pltpu.make_async_remote_copy(
                src_ref=ret.at[o, pl.ds(0, slots), at], dst_ref=back.at[o, pl.ds(0, slots), at],
                send_sem=ret_send.at[o, f], recv_sem=ret_recv.at[o, f],
                device_id=member(-o), device_id_type=MESH,
            )
            returns[o, f].start()

    for f in range(feat):
        at = pl.ds(f * step_f, step_f)
        for o in range(n_exp):
            if o > 0:
                returns[o, f].wait_recv()
            rows32[pl.ds(o * slots, slots), :] = back[o, 0:slots, at].astype(jnp.float32)
        rows = rows32[...].astype(jnp.bfloat16)
        mixed = jnp.dot(weights[0, :, 0:total], rows, preferred_element_type=jnp.float32)
        mixed += jnp.dot(weights[1, :, 0:total], rows, preferred_element_type=jnp.float32)
        out_ref[:, at] = (arrived[:, at].astype(jnp.float32) + mixed).astype(jnp.bfloat16)

    for copies in [shifts, dispatch.values(), small_copies, square_copies, returns.values()] + exchange:
        for copy in copies:
            copy.wait_send()


def shards(sizes, stream, expert_ids, norm_gain, router, w_up, w_down):
    n_pipe, n_exp, n_ten = sizes
    tok_rows, width = stream.shape[2:]
    fanout = expert_ids.shape[-1]
    experts = router.shape[2]
    hidden_units = w_up.shape[2]
    tokens = 2 * tok_rows
    capacity = 3 * tok_rows * fanout // (2 * experts)
    slots = -(-2 * capacity // 8) * 8
    total = n_exp * slots
    feat = pieces_of(width, 4)
    cols = pieces_of(hidden_units, 4)
    bf16, f32 = jnp.bfloat16, jnp.float32
    dma = pltpu.SemaphoreType.DMA
    vmem = pl.BlockSpec(memory_space=pltpu.VMEM)
    hbm = pl.BlockSpec(memory_space=pl.ANY)
    result = pl.pallas_call(
        functools.partial(layer, sizes, slots, feat, cols),
        out_shape=jax.ShapeDtypeStruct((tokens, width), bf16),
        in_specs=[hbm, vmem, hbm, vmem, hbm, hbm],
        out_specs=vmem,
        scratch_shapes=[
            pltpu.VMEM((width, hidden_units), bf16),
            pltpu.VMEM((hidden_units, width), bf16),
            pltpu.VMEM((tokens, width), bf16),
            pltpu.VMEM((n_exp, -(-slots // 16) * 16, width), bf16),
            pltpu.VMEM((n_exp, -(-slots // 16) * 16, width), bf16),
            pltpu.VMEM((total, width // feat), f32),
            pltpu.VMEM((total, hidden_units), f32),
            pltpu.VMEM((cols, total, hidden_units // cols), bf16),
            pltpu.VMEM((n_ten, cols, total, hidden_units // cols), bf16),
            pltpu.VMEM((total, hidden_units), bf16),
            pltpu.VMEM((total, 128), f32),
            pltpu.VMEM((n_ten, total, 128), f32),
            pltpu.VMEM((2, tokens, 128), f32),
            pltpu.VMEM((n_ten, 2, tokens, 128), f32),
            pltpu.VMEM((n_exp, -(-slots // 16) * 16, width), bf16),
            pltpu.VMEM((n_exp, -(-slots // 16) * 16, width), bf16),
            pltpu.VMEM((2, tokens, -(-total // 128) * 128), bf16),
            pltpu.VMEM((1, width + 1024), f32),
            dma((feat + 2,)),
            dma((2,)),
            dma((2,)),
            dma((n_exp, feat)),
            dma((n_exp, feat)),
            dma((n_ten, cols + 2)),
            dma((n_ten, cols + 2)),
            dma((n_exp, feat)),
            dma((n_exp, feat)),
        ],
        compiler_params=pltpu.CompilerParams(
            collective_id=0, has_side_effects=True, vmem_limit_bytes=60 * 1024 * 1024
        ),
    )(stream, expert_ids.reshape(tokens, fanout), norm_gain, router[0].T, w_up, w_down)
    return result.reshape(2, 1, tok_rows, width)


def solution(mesh):
    sizes = tuple(mesh.shape[axis] for axis in ("pipe", "expert", "tensor"))
    return jax.shard_map(
        functools.partial(shards, sizes),
        mesh=mesh,
        in_specs=(
            P(None, "pipe", "expert", "tensor"),
            P(None, "pipe", "expert", None),
            P("pipe", "tensor"),
            P("pipe", "tensor", None),
            P("expert", "tensor", None),
            P("expert", None, "tensor"),
        ),
        out_specs=P(None, "pipe", "expert", "tensor"),
        check_vma=False,
    )
```
